32 devices in a mesh: rows: 16 (over z, y, x), heads: 2 (over core).
Axes of the slice: x: 2, y: 2, z: 4, core: 2. Of those that a mesh axis runs over, the one named last changes fastest.
Arguments:
- tokens: bfloat16 [32768, 768], P(('rows', 'heads')), may hold values from -6 to 6
- cotangent: bfloat16 [32768, 768], P(('rows', 'heads')), may hold values from -6 to 6
- segment_ids: int32 [64, 512], P('rows'), may hold values from 0 to 7, never falling along the last dimension, each value on 1 to 256 neighbouring positions
- valid_count: int32 [64], P('rows'), may hold values from 1 to 512, 24576 in all
- qkv_weight: bfloat16 [768, 2304], P(('rows', 'heads')), may hold values from -0.21875 to 0.21875
- qv_bias: bfloat16 [2, 768], P(None, ('rows', 'heads')), may hold values from -0.59765625 to 0.59765625
- out_weight: bfloat16 [768, 768], P(('rows', 'heads')), may hold values from -1.75 to 1.75
- out_bias: bfloat16 [768], P(('rows', 'heads')), may hold values from -1.796875 to 1.796875
- norm_gain: bfloat16 [768], P(('rows', 'heads')), may hold values from 0.5 to 1.5
- norm_shift: bfloat16 [768], P(('rows', 'heads')), may hold values from -1.796875 to 1.796875
- in_weight: bfloat16 [768, 3072], P(('rows', 'heads')), may hold values from -0.21875 to 0.21875
- in_bias: bfloat16 [3072], P(('rows', 'heads')), may hold values from -1.796875 to 1.796875
- back_weight: bfloat16 [3072, 768], P(('rows', 'heads')), may hold values from -0.109375 to 0.109375
- back_bias: bfloat16 [768], P(('rows', 'heads')), may hold values from -1.796875 to 1.796875
- final_gain: bfloat16 [768], P(('rows', 'heads')), may hold values from 0.5 to 1.5
- final_shift: bfloat16 [768], P(('rows', 'heads')), may hold values from -1.796875 to 1.796875
Outputs:
- layer_out: bfloat16 [32768, 768], P(('rows', 'heads'))
- grad_tokens: float32 [32768, 768], P(('rows', 'heads'))
- grad_qkv_weight: float32 [768, 2304], P(('rows', 'heads'))
- grad_qv_bias: float32 [2, 768], P(None, ('rows', 'heads'))
- grad_out_weight: float32 [768, 768], P(('rows', 'heads'))
- grad_out_bias: float32 [768], P(('rows', 'heads'))
- grad_norm_gain: float32 [768], P(('rows', 'heads'))
- grad_norm_shift: float32 [768], P(('rows', 'heads'))
- grad_in_weight: float32 [768, 3072], P(('rows', 'heads'))
- grad_in_bias: float32 [3072], P(('rows', 'heads'))
- grad_back_weight: float32 [3072, 768], P(('rows', 'heads'))
- grad_back_bias: float32 [768], P(('rows', 'heads'))
- grad_final_gain: float32 [768], P(('rows', 'heads'))
- grad_final_shift: float32 [768], P(('rows', 'heads'))
The draws below stay inside these ranges and needn't reach their ends.
Inputs may be any that keep to these rules, and one draw needn't show every extreme that they name: `segment_ids`: along a row the numbers never fall; each segment spans 1 to 256 positions. `valid_count`: the counts of all 64 rows sum to 24576.
All inputs are finite; a program needn't handle non-finite values. No bound on the sum of `valid_count` on one device may be relied on, other than what follows from the above.
Results may differ from the reference program's by a relative error of at most 0.013.
Values may be sent and summed in bfloat16 or wider, within the bound.
No kernel may reach another device: no remote copies, remote signals or barrier semaphores. Data moves between devices by JAX's collectives and lax.ppermute only.
A program may use at most 192 MiB of HBM per device.

```python
import math
import jax
import jax.numpy as jnp
import numpy as np
from jax import lax

D = 768
HEADS = 12
HEAD_DIM = 64
FF = 3072
L = 512
SEG_COUNT = 8
SEQS = 64
TOKENS = 32768


def strengthened(values, key, source, target, shards_of, factor):
    def block_of(position):
        return (jnp.arange(values.shape[position]) // (values.shape[position] // shards_of)).reshape((-1,) + (1,) * (values.ndim - 1 - position))

    near = jax.random.permutation(key, shards_of)[block_of(target)]
    far = (block_of(target) + shards_of // 2) % shards_of
    return jnp.where((block_of(source) == near) | (block_of(source) == far), factor * values, values)


def block_levels(rng, dims, shards, low, largest):
    def one(dim, shards_of):
        steps = jax.random.uniform(jax.random.fold_in(jax.random.fold_in(rng, 6), dim), (shards_of,), jnp.float32, low / len(shards), largest / len(shards))
        return jnp.repeat(jnp.exp(steps), dims[dim] // shards_of).reshape((-1,) + (1,) * (len(dims) - dim - 1))

    loudness = one(*shards[0])
    for cut in shards[1:]:
        loudness = loudness * one(*cut)
    return loudness


def profile(count, total, bound, lean):
    portions = [(1 << 20) // math.isqrt(standing ** lean) + 1 for standing in range(2, count + 1)]
    surplus, given = total - bound - (count - 1), [1] * (count - 1)
    while surplus > 0:
        free = [i for i in range(count - 1) if given[i] < bound]
        whole, budget = sum([portions[i] for i in free]), surplus
        for i in free:
            addition = min(bound - given[i], max(1, budget * portions[i] // whole), surplus)
            given[i] = given[i] + addition
            surplus = surplus - addition
    return np.array([bound] + given)


def uneven(stream_key, count, total, most, skew):
    if count == 2:
        one = jax.random.randint(stream_key, (), max(1, total - most), min(most, total - 1) + 1)
        return jnp.stack([one, total - one])
    lengths = jnp.asarray(profile(count, total, most, skew), jnp.int32)
    pairs = (count - 1) // 2
    donor, receiver = lengths[1:1 + 2 * pairs:2], lengths[2:2 + 2 * pairs:2]
    margin = jnp.minimum(donor - 1, most - receiver)
    moved = jax.random.randint(jax.random.fold_in(stream_key, 1), (pairs,), 0, 1 << 20) % (margin + 1)
    lengths = lengths.at[1:1 + 2 * pairs:2].set(donor - moved).at[2:2 + 2 * pairs:2].set(receiver + moved)
    return lengths[jax.random.permutation(jax.random.fold_in(stream_key, 2), count)]


def bell_draw(own_key, shape, scale, reach, pieces=(), held_as=jnp.bfloat16):
    drawn = jax.random.normal(own_key, shape, jnp.float32) * scale
    if len(pieces) > 0:
        drawn = block_levels(own_key, shape, pieces, -0.22, 0.18) * drawn
    return jnp.clip(drawn, min=-reach, max=reach).astype(held_as)


def noise_with(stream_key, extent, width, most, split, heavy, kind=jnp.bfloat16):
    result = width * jax.random.normal(stream_key, extent, jnp.float32)
    if split:
        result = result * block_levels(stream_key, extent, split, -0.22, 0.18)
    return jnp.clip(strengthened(result, jax.random.fold_in(stream_key, 3), *heavy), -most, most).astype(kind)


def setup_inputs(seed: int = 0) -> dict:
    splits = jax.random.split(jax.random.key(seed), 17)
    return {
        "tokens": bell_draw(splits[0], (TOKENS, D), 1.0, 6.0, ((0, 32),)),
        "cotangent": noise_with(splits[1], (TOKENS, D), 1.0, 6.0, ((0, 32),), (0, 1, 32, 2.75)),
        "segment_ids": jax.vmap(lambda own: jnp.searchsorted(jnp.cumsum(uneven(own, SEG_COUNT, L, L // 2, 1)), jnp.arange(L), side="right"))(jax.random.split(splits[2], SEQS)).reshape((SEQS, L)).astype(jnp.int32),
        "valid_count": uneven(splits[3], SEQS, SEQS * 3 * L // 4, L, 1).astype(jnp.int32),
        "qkv_weight": bell_draw(splits[4], (D, 3 * D), D ** -0.5, 0.21875, ((0, 32),)),
        "qv_bias": bell_draw(splits[5], (2, D), 0.1, 0.59765625, ((1, 32),)),
        "out_weight": bell_draw(splits[6], (D, D), (D // 64) ** -0.5, 1.75, ((0, 32),)),
        "out_bias": bell_draw(splits[7], (D,), 0.3, 1.796875, ((0, 32),)),
        "norm_gain": jnp.clip(1.0 + 0.1 * jax.random.normal(splits[8], (D,), jnp.float32), 0.5, 1.5).astype(jnp.bfloat16),
        "norm_shift": bell_draw(splits[9], (D,), 0.3, 1.796875, ((0, 32),)),
        "in_weight": bell_draw(splits[10], (D, FF), D ** -0.5, 0.21875, ((0, 32),)),
        "in_bias": bell_draw(splits[11], (FF,), 0.3, 1.796875, ((0, 32),)),
        "back_weight": bell_draw(splits[12], (FF, D), FF ** -0.5, 0.109375, ((0, 32),)),
        "back_bias": bell_draw(splits[13], (D,), 0.3, 1.796875, ((0, 32),)),
        "final_gain": jnp.clip(1.0 + 0.1 * jax.random.normal(splits[14], (D,), jnp.float32), 0.5, 1.5).astype(jnp.bfloat16),
        "final_shift": bell_draw(splits[15], (D,), 0.3, 1.796875, ((0, 32),)),
    }


@jax.custom_vjp
def low(v):
    return lax.optimization_barrier(v.astype(jnp.bfloat16)).astype(jnp.float32)

@jax.custom_vjp
def low_back(v):
    return v

def low_keep(v):
    return (low(v), None)

def low_pass(kept, grad):
    return (grad,)

def back_keep(v):
    return (v, None)

def back_low(kept, grad):
    return (low(grad),)
low.defvjp(low_keep, low_pass)
low_back.defvjp(back_keep, back_low)
epsilon = 1e-12
highest = lax.Precision.HIGHEST

def layer_norm(values, gain_row, shift_row):
    centered = values - lax.optimization_barrier(jnp.mean(values, axis=-1, keepdims=True))
    variance = lax.optimization_barrier(jnp.mean(centered * centered, axis=-1, keepdims=True))
    return centered * lax.rsqrt(variance + epsilon) * gain_row + shift_row

def attend_row(query_rows, key_rows, value_rows, segment_row, count_row):
    positions = jnp.arange(L)
    same_segment = segment_row[:, None] == segment_row[None, :]
    allowed = same_segment & (positions[None, :] < count_row) | (positions[:, None] == positions[None, :])
    scores = jnp.einsum('qhd,khd->hqk', query_rows, key_rows, precision=highest) * HEAD_DIM ** (-0.5)
    scores = low_back(scores)
    scores = jnp.where(allowed[None], scores, -1e+30)
    weights_soft = jax.nn.softmax(scores, axis=-1)
    weights_low = low(weights_soft)
    return jnp.einsum('hqk,khd->qhd', weights_low, value_rows, precision=highest)
attend_saved = jax.checkpoint(attend_row)

def forward(inputs, params, segment_block, count_block):
    qkv_weight, qv_bias, out_weight, out_bias, norm_gain, norm_shift, in_weight, in_bias, back_weight, back_bias, final_gain, final_shift = params
    group_rows = segment_block.shape[0]
    bias_full = jnp.concatenate([qv_bias[0], jnp.zeros_like(qv_bias[0]), qv_bias[1]])
    projected = jnp.dot(inputs, qkv_weight, precision=highest) + bias_full
    projected = low_back(low(projected)).reshape(group_rows, L, 3, HEADS, HEAD_DIM)
    context = lax.map(lambda block_item: attend_saved(*block_item), (projected[:, :, 0], projected[:, :, 1], projected[:, :, 2], segment_block, count_block))
    context = low_back(low(context.reshape(group_rows * L, D)))
    attn = low_back(jnp.dot(context, out_weight, precision=highest) + out_bias)
    hidden = layer_norm(inputs + attn, norm_gain, norm_shift)
    preactive = low_back(jnp.dot(low(hidden), in_weight, precision=highest) + in_bias)
    activation = low(jax.nn.gelu(preactive, approximate=False))
    feed_out = low_back(jnp.dot(activation, back_weight, precision=highest) + back_bias)
    normed = layer_norm(hidden + feed_out, final_gain, final_shift)
    positions = jnp.arange(L)
    valid_tokens = (positions[None, :] < count_block[:, None]).astype(inputs.dtype).reshape(group_rows * L, 1)
    return normed * valid_tokens

def reference(tokens, cotangent, segment_ids, valid_count, qkv_weight, qv_bias, out_weight, out_bias, norm_gain, norm_shift, in_weight, in_bias, back_weight, back_bias, final_gain, final_shift):
    params = tuple((weight_item.astype(jnp.float32) for weight_item in (qkv_weight, qv_bias, out_weight, out_bias, norm_gain, norm_shift, in_weight, in_bias, back_weight, back_bias, final_gain, final_shift)))
    group_rows = math.gcd(SEQS, max(1, 4096 // L))
    blocks = SEQS // group_rows
    token_blocks = tokens.astype(jnp.float32).reshape(blocks, group_rows * L, D)
    cotangent_blocks = cotangent.astype(jnp.float32).reshape(blocks, group_rows * L, D)
    segment_blocks = segment_ids.reshape(blocks, group_rows, L)
    count_blocks = valid_count.reshape(blocks, group_rows)

    def scan_step(totals, block_item):
        inputs, cotangent_block, segment_block, count_block = block_item
        out_block, pullback = jax.vjp(lambda values_in, params_in: forward(values_in, params_in, segment_block, count_block), inputs, params)
        grad_inputs, grad_params = pullback(cotangent_block)
        return (jax.tree.map(jnp.add, totals, grad_params), (out_block, grad_inputs))
    zero_grads = jax.tree.map(jnp.zeros_like, params)
    totals, (outputs, input_grads) = lax.scan(scan_step, zero_grads, (token_blocks, cotangent_blocks, segment_blocks, count_blocks))
    grad_qkv, grad_qv, grad_out, grad_out_b, grad_gain, grad_shift, grad_in, grad_in_b, grad_back, grad_back_b, grad_final_g, grad_final_s = totals
    return (outputs.reshape(TOKENS, D).astype(jnp.bfloat16), input_grads.reshape(TOKENS, D), grad_qkv, grad_qv, grad_out, grad_out_b, grad_gain, grad_shift, grad_in, grad_in_b, grad_back, grad_back_b, grad_final_g, grad_final_s)
```

```python
import math

import jax
import jax.numpy as jnp
from jax import lax
from jax.sharding import PartitionSpec as P

HEADS = 12
HEAD_DIM = 64
EPS = 1e-12
AXES = ("rows", "heads")
F32 = jnp.float32
BF16 = jnp.bfloat16


def norm_forward(values, gain_row, shift_row):
    centered = values - jnp.mean(values, axis=-1, keepdims=True)
    inverse = lax.rsqrt(jnp.mean(centered * centered, axis=-1, keepdims=True) + EPS)
    normalized = centered * inverse
    return (normalized * gain_row + shift_row, normalized, inverse)


def norm_backward(grad_output, normalized, inverse, gain_row):
    grad_normed = grad_output * gain_row
    grad_input = inverse * (
        grad_normed
        - jnp.mean(grad_normed, axis=-1, keepdims=True)
        - normalized * jnp.mean(grad_normed * normalized, axis=-1, keepdims=True)
    )
    return (grad_input, jnp.sum(grad_output * normalized, axis=0), jnp.sum(grad_output, axis=0))


def allowed_keys(segment_row, count_row):
    positions = jnp.arange(segment_row.shape[0])
    same_segment = segment_row[:, None] == segment_row[None, :]
    return same_segment & (positions[None, :] < count_row) | (
        positions[:, None] == positions[None, :]
    )


def masked_scores(query_rows, key_rows, allowed):
    scores = jnp.einsum(
        "qhd,khd->hqk", query_rows, key_rows, preferred_element_type=F32
    ) * HEAD_DIM ** (-0.5)
    return jnp.where(allowed[None], scores, -1e30)


def attend_forward(query_rows, key_rows, value_rows, segment_row, count_row):
    scores = masked_scores(query_rows, key_rows, allowed_keys(segment_row, count_row))
    highest = jnp.max(scores, axis=-1, keepdims=True)
    exponent = jnp.exp(scores - highest)
    total = jnp.sum(exponent, axis=-1, keepdims=True)
    low = (exponent / total).astype(BF16)
    context = jnp.einsum("hqk,khd->qhd", low, value_rows, preferred_element_type=F32)
    return (context.astype(BF16), (highest + jnp.log(total))[..., 0])


def attend_backward(query_rows, key_rows, value_rows, segment_row, count_row, lse, grad_context):
    scores = masked_scores(query_rows, key_rows, allowed_keys(segment_row, count_row))
    soft = jnp.exp(scores - lse[..., None])
    low = soft.astype(BF16)
    grad_value = jnp.einsum("hqk,qhd->khd", low, grad_context, preferred_element_type=F32)
    grad_soft = jnp.einsum("qhd,khd->hqk", grad_context, value_rows, preferred_element_type=F32)
    inner = jnp.sum(soft * grad_soft, axis=-1, keepdims=True)
    grad_scores = (soft * (grad_soft - inner)).astype(BF16)
    scaling = HEAD_DIM ** (-0.5)
    grad_query = (
        jnp.einsum("hqk,khd->qhd", grad_scores, key_rows, preferred_element_type=F32) * scaling
    )
    grad_key = (
        jnp.einsum("hqk,qhd->khd", grad_scores, query_rows, preferred_element_type=F32) * scaling
    )
    return tuple(g.astype(BF16) for g in (grad_query, grad_key, grad_value))


def local(
    tokens, cotangent, segment_ids, valid_count, qkv_weight, qv_bias, out_weight, out_bias,
    norm_gain, norm_shift, in_weight, in_bias, back_weight, back_bias, final_gain, final_shift,
):
    head_index = lax.axis_index("heads")
    devices = lax.axis_size("rows") * lax.axis_size("heads")
    token_count, width = tokens.shape
    row_length = segment_ids.shape[1]
    rows = token_count // row_length
    shard = qkv_weight.shape[0]
    small = [qv_bias[0], qv_bias[1], out_bias, norm_gain, norm_shift, in_bias, back_bias,
             final_gain, final_shift]
    sizes = [s.shape[0] for s in small]
    total = sum(sizes)
    lanes = -(-total // (shard * 128)) * 128
    packed = jnp.pad(jnp.concatenate(small), (0, shard * lanes - total)).reshape(shard, lanes)
    first = lax.all_gather(
        jnp.concatenate([qkv_weight, packed], axis=1), AXES, axis=0, tiled=True
    )
    qkv_all = first[:, : 3 * width]
    vectors = first[:, 3 * width :].reshape(devices, shard * lanes)
    parts = []
    at = 0
    for n in sizes:
        parts.append(vectors[:, at : at + n].reshape(devices * n).astype(F32))
        at += n
    (q_bias, v_bias, out_bias_f, gain_f, shift_f, in_bias_f, back_bias_f, fgain_f, fshift_f) = parts
    second = lax.all_gather(
        jnp.concatenate([out_weight, in_weight], axis=1), AXES, axis=0, tiled=True
    )
    out_all = second[:, :width]
    in_all = second[:, width:]
    back_all = lax.all_gather(back_weight, AXES, axis=0, tiled=True)

    segments = lax.dynamic_slice(segment_ids, (head_index * rows, 0), (rows, row_length))
    counts = lax.dynamic_slice(valid_count, (head_index * rows,), (rows,))
    bias_full = jnp.concatenate([q_bias, jnp.zeros_like(q_bias), v_bias])
    projected = (jnp.dot(tokens, qkv_all, preferred_element_type=F32) + bias_full).astype(BF16)
    heads = projected.reshape(rows, row_length, 3, HEADS, HEAD_DIM)
    contexts = [
        attend_forward(heads[r, :, 0], heads[r, :, 1], heads[r, :, 2], segments[r], counts[r])
        for r in range(rows)
    ]
    context = jnp.concatenate([c[0].reshape(row_length, width) for c in contexts], axis=0)
    valid = (
        (jnp.arange(row_length)[None, :] < counts[:, None]).astype(F32).reshape(token_count, 1)
    )
    attn = jnp.dot(context, out_all, preferred_element_type=F32) + out_bias_f
    hidden, n1, r1 = norm_forward(tokens.astype(F32) + attn, gain_f, shift_f)
    hidden_low = hidden.astype(BF16)
    preact = jnp.dot(hidden_low, in_all, preferred_element_type=F32) + in_bias_f
    cdf = 0.5 + 0.5 * lax.erf(preact * (0.5 ** 0.5))
    activation = (preact * cdf).astype(BF16)
    slope = (cdf + preact * jnp.exp(-0.5 * preact * preact) * (1.0 / math.sqrt(2 * math.pi))).astype(BF16)
    feed = jnp.dot(activation, back_all, preferred_element_type=F32) + back_bias_f
    finished, n2, r2 = norm_forward(hidden + feed, fgain_f, fshift_f)
    layer_out = (finished * valid).astype(BF16)
    grad_final = cotangent.astype(F32) * valid
    g_res2, g_fgain, g_fshift = norm_backward(grad_final, n2, r2, fgain_f)
    g_ffn = g_res2.astype(BF16)
    g_back_bias = jnp.sum(g_ffn.astype(F32), axis=0)
    g_back = jnp.einsum("tf,td->fd", activation, g_ffn, preferred_element_type=F32).astype(BF16)
    g_back = lax.psum_scatter(g_back, AXES, scatter_dimension=0, tiled=True)
    g_act = jnp.einsum("td,fd->tf", g_ffn, back_all, preferred_element_type=F32)
    g_pre = (g_act * slope.astype(F32)).astype(BF16)
    g_in_bias = jnp.sum(g_pre.astype(F32), axis=0)
    g_in = jnp.einsum("td,tf->df", hidden_low, g_pre, preferred_element_type=F32).astype(BF16)
    g_hidden = g_res2 + jnp.einsum("tf,df->td", g_pre, in_all, preferred_element_type=F32)
    g_res1, g_gain, g_shift = norm_backward(g_hidden, n1, r1, gain_f)
    g_attn = g_res1.astype(BF16)
    g_out_bias = jnp.sum(g_attn.astype(F32), axis=0)
    g_out = jnp.einsum("tc,td->cd", context, g_attn, preferred_element_type=F32).astype(BF16)
    g_oi = lax.psum_scatter(
        jnp.concatenate([g_out, g_in], axis=1), AXES, scatter_dimension=0, tiled=True
    )
    g_context = jnp.einsum("td,cd->tc", g_attn, out_all, preferred_element_type=F32).astype(BF16)
    g_heads = g_context.reshape(rows, row_length, HEADS, HEAD_DIM)
    grads = [
        attend_backward(heads[r, :, 0], heads[r, :, 1], heads[r, :, 2], segments[r], counts[r],
                        contexts[r][1], g_heads[r])
        for r in range(rows)
    ]
    g_proj = jnp.concatenate(
        [jnp.concatenate([g.reshape(row_length, width) for g in row], axis=1) for row in grads],
        axis=0,
    )
    g_qkv = jnp.einsum("td,tc->dc", tokens, g_proj, preferred_element_type=F32).astype(BF16)
    sums = jnp.sum(g_proj.astype(F32), axis=0).reshape(3, width)
    g_small = [sums[0], sums[2], g_out_bias, g_gain, g_shift, g_in_bias, g_back_bias, g_fgain,
               g_fshift]
    g_packed = jnp.concatenate([g.reshape(devices, -1) for g in g_small], axis=1)
    g_packed = jnp.pad(g_packed, ((0, 0), (0, shard * lanes - total))).astype(BF16)
    g_last = lax.psum_scatter(
        jnp.concatenate([g_qkv, g_packed.reshape(devices * shard, lanes)], axis=1),
        AXES, scatter_dimension=0, tiled=True,
    )
    grad_tokens = g_res1 + jnp.einsum("tc,dc->td", g_proj, qkv_all, preferred_element_type=F32)
    mine = g_last[:, 3 * width :].reshape(shard * lanes).astype(F32)
    own = []
    at = 0
    for n in sizes:
        own.append(mine[at : at + n])
        at += n
    return (
        layer_out, grad_tokens, g_last[:, : 3 * width].astype(F32), jnp.stack([own[0], own[1]]),
        g_oi[:, :width].astype(F32), own[2], own[3], own[4], g_oi[:, width:].astype(F32), own[5],
        g_back.astype(F32), own[6], own[7], own[8],
    )


def solution(mesh):
    both = P(AXES, None)
    vec = P(AXES)
    in_specs = (both, both, P("rows", None), P("rows"), both, P(None, AXES), both, vec, vec, vec,
                both, vec, both, vec, vec, vec)
    out_specs = (both, both, both, P(None, AXES), both, vec, vec, vec, both, vec, both, vec, vec,
                 vec)
    return jax.shard_map(local, mesh=mesh, in_specs=in_specs, out_specs=out_specs, check_vma=False)
```

```python
import math

import jax
import jax.numpy as jnp
from jax import lax
from jax.sharding import PartitionSpec as P

HEADS = 12
HEAD_DIM = 64
EPS = 1e-12
AXES = ("rows", "heads")
F32 = jnp.float32
BF16 = jnp.bfloat16


def norm_forward(values, gain_row, shift_row):
    centered = values - jnp.mean(values, axis=-1, keepdims=True)
    inverse = lax.rsqrt(jnp.mean(centered * centered, axis=-1, keepdims=True) + EPS)
    normalized = centered * inverse
    return (normalized * gain_row + shift_row, normalized, inverse)


def norm_backward(grad_output, normalized, inverse, gain_row):
    grad_normed = grad_output * gain_row
    grad_input = inverse * (
        grad_normed
        - jnp.mean(grad_normed, axis=-1, keepdims=True)
        - normalized * jnp.mean(grad_normed * normalized, axis=-1, keepdims=True)
    )
    return (grad_input, jnp.sum(grad_output * normalized, axis=0), jnp.sum(grad_output, axis=0))


def allowed_keys(segment_row, count_row):
    positions = jnp.arange(segment_row.shape[0])
    same_segment = segment_row[:, None] == segment_row[None, :]
    return same_segment & (positions[None, :] < count_row) | (
        positions[:, None] == positions[None, :]
    )


def masked_scores(query_rows, key_rows, allowed):
    scores = jnp.einsum(
        "qhd,khd->hqk", query_rows, key_rows, preferred_element_type=F32
    ) * HEAD_DIM ** (-0.5)
    return jnp.where(allowed[None], scores, -1e30)


def attend_forward(query_rows, key_rows, value_rows, segment_row, count_row):
    scores = masked_scores(query_rows, key_rows, allowed_keys(segment_row, count_row))
    highest = jnp.max(scores, axis=-1, keepdims=True)
    exponent = jnp.exp(scores - highest)
    total = jnp.sum(exponent, axis=-1, keepdims=True)
    low = (exponent / total).astype(BF16)
    context = jnp.einsum("hqk,khd->qhd", low, value_rows, preferred_element_type=F32)
    return (context.astype(BF16), (highest + jnp.log(total))[..., 0])


def attend_backward(query_rows, key_rows, value_rows, segment_row, count_row, lse, grad_context):
    scores = masked_scores(query_rows, key_rows, allowed_keys(segment_row, count_row))
    soft = jnp.exp(scores - lse[..., None])
    low = soft.astype(BF16)
    grad_value = jnp.einsum("hqk,qhd->khd", low, grad_context, preferred_element_type=F32)
    grad_soft = jnp.einsum("qhd,khd->hqk", grad_context, value_rows, preferred_element_type=F32)
    inner = jnp.sum(soft * grad_soft, axis=-1, keepdims=True)
    grad_scores = (soft * (grad_soft - inner)).astype(BF16)
    scaling = HEAD_DIM ** (-0.5)
    grad_query = (
        jnp.einsum("hqk,khd->qhd", grad_scores, key_rows, preferred_element_type=F32) * scaling
    )
    grad_key = (
        jnp.einsum("hqk,qhd->khd", grad_scores, query_rows, preferred_element_type=F32) * scaling
    )
    return tuple(g.astype(BF16) for g in (grad_query, grad_key, grad_value))


def exchange(value, bit, devices):
    return lax.ppermute(value, AXES, [(i, i ^ bit) for i in range(devices)])


def bits_of(devices):
    found, bit = [], devices // 2
    while bit:
        found.append(bit)
        bit //= 2
    return found


def orders_of(devices):
    high = [b for b in bits_of(devices) if b >= 8]
    return ([1, 2, 4] + high[::-1], [1, 4, 2] + high[::-1])


def pick(value, index, axis):
    return lax.dynamic_index_in_dim(value, index, axis, keepdims=False)


def scatter_sum(grad, me, devices, cuts):
    rows = grad.shape[0] // devices
    bits = bits_of(devices)
    whole = grad.reshape((2,) * len(bits) + (rows, grad.shape[1]))
    axis = len(bits) - 1
    mine = me & 1
    got = exchange(pick(whole, 1 - mine, axis), 1, devices)
    half = pick(whole, mine, axis).astype(F32) + got.astype(F32)
    outs = []
    for order, (start, stop) in zip(orders_of(devices), cuts):
        state = half[..., start:stop]
        left = [b for b in bits if b != 1]
        for bit in order[1:]:
            axis = left.index(bit)
            left.remove(bit)
            mine = (me // bit) & 1
            low = state.astype(BF16)
            got = exchange(pick(low, 1 - mine, axis), bit, devices)
            state = pick(low, mine, axis).astype(F32) + got.astype(F32)
        outs.append(state)
    return outs[0] if len(outs) == 1 else jnp.concatenate(outs, axis=1)


def gather_rows(shard, me, devices, cuts):
    bits = bits_of(devices)
    outs = []
    for order, (start, stop) in zip(orders_of(devices), cuts):
        state = shard[:, start:stop]
        done = []
        for bit in order[::-1]:
            got = exchange(state, bit, devices)
            axis = sum(1 for b in done if b > bit)
            done.append(bit)
            mine = ((me // bit) & 1) == 0
            state = jnp.stack(
                [jnp.where(mine, state, got), jnp.where(mine, got, state)], axis=axis
            )
        outs.append(state.reshape(devices * shard.shape[0], stop - start))
    return outs


def local(
    tokens, cotangent, segment_ids, valid_count, qkv_weight, qv_bias, out_weight, out_bias,
    norm_gain, norm_shift, in_weight, in_bias, back_weight, back_bias, final_gain, final_shift,
):
    head_index = lax.axis_index("heads")
    devices = lax.axis_size("rows") * lax.axis_size("heads")
    token_count, width = tokens.shape
    row_length = segment_ids.shape[1]
    rows = token_count // row_length
    shard = qkv_weight.shape[0]
    small = [qv_bias[0], qv_bias[1], out_bias, norm_gain, norm_shift, in_bias, back_bias,
             final_gain, final_shift]
    sizes = [s.shape[0] for s in small]
    total = sum(sizes)
    lanes = -(-total // (shard * 128)) * 128
    packed = jnp.pad(jnp.concatenate(small), (0, shard * lanes - total)).reshape(shard, lanes)
    me = lax.axis_index("rows") * lax.axis_size("heads") + head_index
    joined = jnp.concatenate([qkv_weight, packed], axis=1)
    half = (joined.shape[1] // 256) * 128
    butterfly = shard % 8 == 0 and devices & (devices - 1) == 0 and devices >= 8

    def reduce_to_owner(grad, cuts):
        if butterfly:
            return scatter_sum(grad, me, devices, cuts)
        return lax.psum_scatter(grad, AXES, scatter_dimension=0, tiled=True).astype(F32)

    if butterfly:
        first = jnp.concatenate(
            gather_rows(joined, me, devices, ((0, half), (half, joined.shape[1]))), axis=1
        )
    else:
        first = lax.all_gather(joined, AXES, axis=0, tiled=True)
    qkv_all = first[:, : 3 * width]
    vectors = first[:, 3 * width :].reshape(devices, shard * lanes)
    parts = []
    at = 0
    for n in sizes:
        parts.append(vectors[:, at : at + n].reshape(devices * n).astype(F32))
        at += n
    (q_bias, v_bias, out_bias_f, gain_f, shift_f, in_bias_f, back_bias_f, fgain_f, fshift_f) = parts
    second = lax.all_gather(
        jnp.concatenate([out_weight, in_weight], axis=1), AXES, axis=0, tiled=True
    )
    out_all = second[:, :width]
    in_all = second[:, width:]
    back_all = lax.all_gather(back_weight, AXES, axis=0, tiled=True)

    segments = lax.dynamic_slice(segment_ids, (head_index * rows, 0), (rows, row_length))
    counts = lax.dynamic_slice(valid_count, (head_index * rows,), (rows,))
    bias_full = jnp.concatenate([q_bias, jnp.zeros_like(q_bias), v_bias])
    projected = (jnp.dot(tokens, qkv_all, preferred_element_type=F32) + bias_full).astype(BF16)
    heads = projected.reshape(rows, row_length, 3, HEADS, HEAD_DIM)
    contexts = [
        attend_forward(heads[r, :, 0], heads[r, :, 1], heads[r, :, 2], segments[r], counts[r])
        for r in range(rows)
    ]
    context = jnp.concatenate([c[0].reshape(row_length, width) for c in contexts], axis=0)
    valid = (
        (jnp.arange(row_length)[None, :] < counts[:, None]).astype(F32).reshape(token_count, 1)
    )
    attn = jnp.dot(context, out_all, preferred_element_type=F32) + out_bias_f
    hidden, n1, r1 = norm_forward(tokens.astype(F32) + attn, gain_f, shift_f)
    hidden_low = hidden.astype(BF16)
    preact = jnp.dot(hidden_low, in_all, preferred_element_type=F32) + in_bias_f
    cdf = 0.5 + 0.5 * lax.erf(preact * (0.5 ** 0.5))
    activation = (preact * cdf).astype(BF16)
    slope = (cdf + preact * jnp.exp(-0.5 * preact * preact) * (1.0 / math.sqrt(2 * math.pi))).astype(BF16)
    feed = jnp.dot(activation, back_all, preferred_element_type=F32) + back_bias_f
    finished, n2, r2 = norm_forward(hidden + feed, fgain_f, fshift_f)
    layer_out = (finished * valid).astype(BF16)
    grad_final = cotangent.astype(F32) * valid
    g_res2, g_fgain, g_fshift = norm_backward(grad_final, n2, r2, fgain_f)
    g_ffn = g_res2.astype(BF16)
    g_back_bias = jnp.sum(g_ffn.astype(F32), axis=0)
    g_back = jnp.einsum("tf,td->fd", activation, g_ffn, preferred_element_type=F32).astype(BF16)
    g_back = reduce_to_owner(g_back, ((0, width // 2), (width // 2, width)))
    g_act = jnp.einsum("td,fd->tf", g_ffn, back_all, preferred_element_type=F32)
    g_pre = (g_act * slope.astype(F32)).astype(BF16)
    g_in_bias = jnp.sum(g_pre.astype(F32), axis=0)
    g_in = jnp.einsum("td,tf->df", hidden_low, g_pre, preferred_element_type=F32).astype(BF16)
    g_hidden = g_res2 + jnp.einsum("tf,df->td", g_pre, in_all, preferred_element_type=F32)
    g_res1, g_gain, g_shift = norm_backward(g_hidden, n1, r1, gain_f)
    g_attn = g_res1.astype(BF16)
    g_out_bias = jnp.sum(g_attn.astype(F32), axis=0)
    g_out = jnp.einsum("tc,td->cd", context, g_attn, preferred_element_type=F32).astype(BF16)
    g_oi = jnp.concatenate([g_out, g_in], axis=1)
    g_oi = reduce_to_owner(g_oi, ((0, g_oi.shape[1] // 2), (g_oi.shape[1] // 2, g_oi.shape[1])))
    g_context = jnp.einsum("td,cd->tc", g_attn, out_all, preferred_element_type=F32).astype(BF16)
    g_heads = g_context.reshape(rows, row_length, HEADS, HEAD_DIM)
    grads = [
        attend_backward(heads[r, :, 0], heads[r, :, 1], heads[r, :, 2], segments[r], counts[r],
                        contexts[r][1], g_heads[r])
        for r in range(rows)
    ]
    g_proj = jnp.concatenate(
        [jnp.concatenate([g.reshape(row_length, width) for g in row], axis=1) for row in grads],
        axis=0,
    )
    g_qkv = jnp.einsum("td,tc->dc", tokens, g_proj, preferred_element_type=F32).astype(BF16)
    sums = jnp.sum(g_proj.astype(F32), axis=0).reshape(3, width)
    g_small = [sums[0], sums[2], g_out_bias, g_gain, g_shift, g_in_bias, g_back_bias, g_fgain,
               g_fshift]
    g_packed = jnp.concatenate([g.reshape(devices, -1) for g in g_small], axis=1)
    g_packed = jnp.pad(g_packed, ((0, 0), (0, shard * lanes - total))).astype(BF16)
    g_last = reduce_to_owner(
        jnp.concatenate([g_qkv, g_packed.reshape(devices * shard, lanes)], axis=1),
        ((0, half), (half, joined.shape[1])),
    )
    grad_tokens = g_res1 + jnp.einsum("tc,dc->td", g_proj, qkv_all, preferred_element_type=F32)
    mine = g_last[:, 3 * width :].reshape(shard * lanes).astype(F32)
    own = []
    at = 0
    for n in sizes:
        own.append(mine[at : at + n])
        at += n
    return (
        layer_out, grad_tokens, g_last[:, : 3 * width].astype(F32), jnp.stack([own[0], own[1]]),
        g_oi[:, :width].astype(F32), own[2], own[3], own[4], g_oi[:, width:].astype(F32), own[5],
        g_back.astype(F32), own[6], own[7], own[8],
    )


def solution(mesh):
    both = P(AXES, None)
    vec = P(AXES)
    in_specs = (both, both, P("rows", None), P("rows"), both, P(None, AXES), both, vec, vec, vec,
                both, vec, both, vec, vec, vec)
    out_specs = (both, both, both, P(None, AXES), both, vec, vec, vec, both, vec, both, vec, vec,
                 vec)
    return jax.shard_map(local, mesh=mesh, in_specs=in_specs, out_specs=out_specs, check_vma=False)
```

```python
import math
from functools import partial

import jax
import jax.numpy as jnp
from jax import lax
from jax.experimental import pallas as pl
from jax.experimental.pallas import tpu as pltpu
from jax.sharding import PartitionSpec as P

HEADS = 12
HEAD_DIM = 64
EPS = 1e-12
NEG = -1e30
AXES = ("rows", "heads")
F32 = jnp.float32
BF16 = jnp.bfloat16
NT = (((1,), (1,)), ((), ()))
NN = (((1,), (0,)), ((), ()))


def dot(a, b, dims=NN):
    return lax.dot_general(a, b, dims, preferred_element_type=F32)


def fill_mask(bias_ref, key_segment, query_segment, count):
    keys = lax.broadcasted_iota(jnp.int32, bias_ref.shape, 0)
    queries = lax.broadcasted_iota(jnp.int32, bias_ref.shape, 1)
    allowed = ((key_segment == query_segment) & (keys < count)) | (keys == queries)
    bias_ref[...] = jnp.where(allowed, 0.0, NEG)


def attend_forward_kernel(count_ref, kseg_ref, qseg_ref, q_ref, k_ref, v_ref, ctx_ref, lse_ref, bias_ref):
    row = pl.program_id(0)

    @pl.when(pl.program_id(1) == 0)
    def _():
        fill_mask(bias_ref, kseg_ref[0], qseg_ref[0], count_ref[row])

    for h in range(6):
        cols = slice(h * HEAD_DIM, (h + 1) * HEAD_DIM)
        query = q_ref[:, cols] * BF16(HEAD_DIM**-0.5)
        scores = dot(k_ref[:, cols], query, NT) + bias_ref[...]
        top = jnp.max(scores, axis=0, keepdims=True)
        exponent = jnp.exp(scores - top)
        total = jnp.sum(exponent, axis=0, keepdims=True)
        inverse = jnp.broadcast_to(1.0 / total, (HEAD_DIM, 512)).T
        context = dot(exponent.astype(BF16), v_ref[:, cols], (((0,), (0,)), ((), ())))
        ctx_ref[:, cols] = (context * inverse).astype(BF16)
        lse_ref[0, 0, h : h + 1, :] = top + jnp.log(total)


def attend_forward(proj, segments, counts):
    tokens, columns = proj.shape
    rows, length = segments.shape
    width = columns // 3
    pairs = width // 384
    block = lambda shift: pl.BlockSpec((length, 384), lambda r, p, c: (r, shift * pairs + p))
    return pl.pallas_call(
        attend_forward_kernel,
        grid_spec=pltpu.PrefetchScalarGridSpec(
            num_scalar_prefetch=1,
            grid=(rows, pairs),
            in_specs=[
                pl.BlockSpec((1, length, 1), lambda r, p, c: (r, 0, 0)),
                pl.BlockSpec((1, 1, length), lambda r, p, c: (r, 0, 0)),
                block(0), block(1), block(2),
            ],
            out_specs=[
                pl.BlockSpec((length, 384), lambda r, p, c: (r, p)),
                pl.BlockSpec((1, 1, 6, length), lambda r, p, c: (r, p, 0, 0)),
            ],
            scratch_shapes=[pltpu.VMEM((length, length), F32)],
        ),
        out_shape=[
            jax.ShapeDtypeStruct((tokens, width), BF16),
            jax.ShapeDtypeStruct((rows, pairs, 6, length), F32),
        ],
        cost_estimate=pl.CostEstimate(flops=8 * tokens * length * width, transcendentals=tokens * length * 12,
                                      bytes_accessed=8 * tokens * width),
        name="attend_forward",
    )(counts, segments[:, :, None], segments[:, None, :], proj, proj, proj)


def attend_backward_kernel(count_ref, kseg_ref, qseg_ref, q_ref, k_ref, v_ref, ctx_ref, gctx_ref, lse_ref,
                           g_ref, bias_ref):
    row = pl.program_id(0)

    @pl.when(pl.program_id(1) == 0)
    def _():
        fill_mask(bias_ref, kseg_ref[0], qseg_ref[0], count_ref[row])

    key_t = k_ref[...].T
    product_t = (gctx_ref[...].astype(F32) * ctx_ref[...].astype(F32)).T
    scale = HEAD_DIM**-0.5
    for h in range(6):
        cols = slice(h * HEAD_DIM, (h + 1) * HEAD_DIM)
        query = q_ref[:, cols] * BF16(scale)
        scores = dot(k_ref[:, cols], query, NT) + bias_ref[...]
        probs = jnp.exp(scores - lse_ref[0, 0, h : h + 1, :])
        inner = jnp.sum(product_t[cols], axis=0, keepdims=True)
        g_probs = dot(v_ref[:, cols], gctx_ref[:, cols], NT)
        g_scores = (probs * (g_probs - inner)).astype(BF16)
        g_ref[2, :, cols] = dot(probs.astype(BF16), gctx_ref[:, cols]).astype(BF16)
        g_ref[1, :, cols] = dot(g_scores, query).astype(BF16)
        g_ref[0, :, cols] = (dot(key_t[cols], g_scores).T * scale).astype(BF16)


def attend_backward(proj, context, g_context, lse, segments, counts):
    tokens, columns = proj.shape
    rows, length = segments.shape
    width = columns // 3
    pairs = width // 384
    block = lambda shift: pl.BlockSpec((length, 384), lambda r, p, c: (r, shift * pairs + p))
    return pl.pallas_call(
        attend_backward_kernel,
        grid_spec=pltpu.PrefetchScalarGridSpec(
            num_scalar_prefetch=1,
            grid=(rows, pairs),
            in_specs=[
                pl.BlockSpec((1, length, 1), lambda r, p, c: (r, 0, 0)),
                pl.BlockSpec((1, 1, length), lambda r, p, c: (r, 0, 0)),
                block(0), block(1), block(2), block(0), block(0),
                pl.BlockSpec((1, 1, 6, length), lambda r, p, c: (r, p, 0, 0)),
            ],
            out_specs=pl.BlockSpec((3, length, 384), lambda r, p, c: (0, r, p)),
            scratch_shapes=[pltpu.VMEM((length, length), F32)],
        ),
        out_shape=jax.ShapeDtypeStruct((3, tokens, width), BF16),
        cost_estimate=pl.CostEstimate(flops=20 * tokens * length * width, transcendentals=tokens * length * 12,
                                      bytes_accessed=16 * tokens * width),
        name="attend_backward",
    )(counts, segments[:, :, None], segments[:, None, :], proj, proj, proj, context, g_context, lse)


def mean(values):
    return jnp.mean(values, axis=-1, keepdims=True)


def add_rows(ref, rows):
    for i, value in enumerate(rows):
        ref[i : i + 1, :] += jnp.sum(value, axis=0, keepdims=True)


def feed_kernel(length, chunk, count_ref, ctx_ref, tok_ref, cot_ref, vec_ref, inb_ref, outw_ref, inw_ref,
                backw_ref, layer_ref, low_ref, n1_ref, r1_ref, act_ref, gpre_ref, gres_ref, gffn_ref, sums_ref,
                ginb_ref, slope_ref):
    step = pl.program_id(0)
    block = tok_ref.shape[0]
    ff = inw_ref.shape[1]

    @pl.when(step == 0)
    def _():
        sums_ref[...] = jnp.zeros_like(sums_ref)
        ginb_ref[...] = jnp.zeros_like(ginb_ref)

    value = tok_ref[...].astype(F32) + (dot(ctx_ref[...], outw_ref[...]) + vec_ref[0:1])
    centered = value - mean(value)
    r1 = lax.rsqrt(mean(centered * centered) + EPS)
    n1 = centered * r1
    n1_ref[...] = n1.astype(BF16)
    r1_ref[...] = r1
    hidden = n1 * vec_ref[1:2] + vec_ref[2:3]
    low = hidden.astype(BF16)
    low_ref[...] = low
    feed = vec_ref[3:4] + hidden
    for c in range(0, ff, chunk):
        cols = slice(c, c + chunk)
        pre = dot(low, inw_ref[:, cols]) + inb_ref[:, cols]
        cdf = 0.5 + 0.5 * lax.erf(pre * (0.5**0.5))
        act = (pre * cdf).astype(BF16)
        act_ref[:, cols] = act
        bell = jnp.exp(pre * pre * -0.5) * (1.0 / math.sqrt(2 * math.pi))
        slope_ref[:, cols] = (cdf + pre * bell).astype(BF16)
        feed = feed + dot(act, backw_ref[cols, :])
    centered = feed - mean(feed)
    r2 = lax.rsqrt(mean(centered * centered) + EPS)
    n2 = centered * r2
    start = (step * block) % length
    position = start + lax.broadcasted_iota(jnp.int32, (block, 1), 0)
    valid = (position < count_ref[(step * block) // length]).astype(F32)
    layer_ref[...] = ((n2 * vec_ref[4:5] + vec_ref[5:6]) * valid).astype(BF16)
    g_final = cot_ref[...].astype(F32) * valid
    g_n = g_final * vec_ref[4:5]
    g_res = r2 * (g_n - mean(g_n) - n2 * mean(g_n * n2))
    gres_ref[...] = g_res
    g_ffn = g_res.astype(BF16)
    gffn_ref[...] = g_ffn
    add_rows(sums_ref, [g_final * n2, g_final, g_ffn.astype(F32)])
    for c in range(0, ff, chunk):
        cols = slice(c, c + chunk)
        g_act = dot(g_ffn, backw_ref[cols, :], NT)
        g_pre = (g_act * slope_ref[:, cols].astype(F32)).astype(BF16)
        gpre_ref[:, cols] = g_pre
        ginb_ref[0:1, cols] += jnp.sum(g_pre.astype(F32), axis=0, keepdims=True)


def feed_call(context, tokens, cotangent, counts, vectors, in_bias, out_w, in_w, back_w, length, block=256, chunk=768):
    count, width = tokens.shape
    ff = in_w.shape[1]
    row = lambda n, dtype: (pl.BlockSpec((block, n), lambda i, c: (i, 0)), jax.ShapeDtypeStruct((count, n), dtype))
    fixed = lambda a: pl.BlockSpec(a.shape, lambda i, c: (0, 0), pipeline_mode=pl.Buffered(1))
    acc = lambda n: (pl.BlockSpec((8, n), lambda i, c: (0, 0)), jax.ShapeDtypeStruct((8, n), F32))
    outs = [row(width, BF16), row(width, BF16), row(width, BF16), row(1, F32), row(ff, BF16), row(ff, BF16),
            row(width, F32), row(width, BF16), acc(width), acc(ff)]
    tok = row(width, BF16)[0]
    return pl.pallas_call(
        partial(feed_kernel, length, chunk),
        grid_spec=pltpu.PrefetchScalarGridSpec(
            num_scalar_prefetch=1,
            grid=(count // block,),
            in_specs=[tok, tok, tok] + [fixed(a) for a in (vectors, in_bias, out_w, in_w, back_w)],
            out_specs=[o[0] for o in outs],
            scratch_shapes=[pltpu.VMEM((block, ff), BF16)],
        ),
        out_shape=[o[1] for o in outs],
        compiler_params=pltpu.CompilerParams(vmem_limit_bytes=56 << 20),
        cost_estimate=pl.CostEstimate(flops=2 * count * width * (width + 3 * ff), transcendentals=2 * count * ff,
                                      bytes_accessed=2 * count * (8 * width + 2 * ff) + 4 * width * ff),
        name="feed",
    )(counts, context, tokens, cotangent, vectors, in_bias, out_w, in_w, back_w)


def back_kernel(gpre_ref, gres_ref, n1_ref, r1_ref, vec_ref, inw_ref, outw_ref, gres1_ref, gattn_ref, gctx_ref, sums_ref):
    @pl.when(pl.program_id(0) == 0)
    def _():
        sums_ref[...] = jnp.zeros_like(sums_ref)

    g_hidden = gres_ref[...] + dot(gpre_ref[...], inw_ref[...], NT)
    n1 = n1_ref[...].astype(F32)
    g_m = g_hidden * vec_ref[1:2]
    g_res1 = r1_ref[...] * (g_m - mean(g_m) - n1 * mean(g_m * n1))
    gres1_ref[...] = g_res1
    g_attn = g_res1.astype(BF16)
    gattn_ref[...] = g_attn
    gctx_ref[...] = dot(g_attn, outw_ref[...], NT).astype(BF16)
    add_rows(sums_ref, [g_hidden * n1, g_hidden, g_attn.astype(F32)])


def back_call(g_pre, g_res, n1, r1, vectors, in_w, out_w, block=256):
    count, width = g_res.shape
    ff = g_pre.shape[1]
    row = lambda n, dtype: (pl.BlockSpec((block, n), lambda i: (i, 0)), jax.ShapeDtypeStruct((count, n), dtype))
    fixed = lambda a: pl.BlockSpec(a.shape, lambda i: (0, 0), pipeline_mode=pl.Buffered(1))
    outs = [row(width, F32), row(width, BF16), row(width, BF16),
            (pl.BlockSpec((8, width), lambda i: (0, 0)), jax.ShapeDtypeStruct((8, width), F32))]
    return pl.pallas_call(
        back_kernel,
        grid=(count // block,),
        in_specs=[row(ff, BF16)[0], row(width, F32)[0], row(width, BF16)[0], row(1, F32)[0], fixed(vectors), fixed(in_w), fixed(out_w)],
        out_specs=[o[0] for o in outs],
        out_shape=[o[1] for o in outs],
        compiler_params=pltpu.CompilerParams(vmem_limit_bytes=48 << 20),
        cost_estimate=pl.CostEstimate(flops=2 * count * width * (width + ff), transcendentals=0,
                                      bytes_accessed=2 * count * (8 * width + ff) + 2 * width * ff),
        name="back",
    )(g_pre, g_res, n1, r1, vectors, in_w, out_w)


def weight_grad_kernel(left_ref, right_ref, out_ref, turned_ref):
    @pl.when(pl.program_id(0) == 0)
    def _():
        turned_ref[...] = left_ref[...].T

    out_ref[...] = dot(turned_ref[...], right_ref[0]).astype(BF16)


def weight_grad(left, right):
    count, rows = left.shape
    parts, _, columns = right.shape
    return pl.pallas_call(
        weight_grad_kernel,
        grid=(parts,),
        in_specs=[pl.BlockSpec((count, rows), lambda k: (0, 0), pipeline_mode=pl.Buffered(1)),
                  pl.BlockSpec((1, count, columns), lambda k: (k, 0, 0))],
        out_specs=pl.BlockSpec((rows, columns), lambda k: (0, k)),
        out_shape=jax.ShapeDtypeStruct((rows, parts * columns), BF16),
        scratch_shapes=[pltpu.VMEM((rows, count), BF16)],
        cost_estimate=pl.CostEstimate(flops=2 * count * rows * parts * columns, transcendentals=0,
                                      bytes_accessed=2 * (count * rows + (count + rows) * parts * columns)),
        name="weight_grad",
    )(left, right)


def token_grad_kernel(grad_ref, weight_ref, rest_ref, out_ref):
    total = rest_ref[...]
    width = rest_ref.shape[1]
    for k in range(grad_ref.shape[0]):
        total = total + dot(grad_ref[k], weight_ref[:, k * width : (k + 1) * width], NT)
    out_ref[...] = total


def token_grad(grad, weight, rest, block=256):
    parts, count, width = grad.shape
    return pl.pallas_call(
        token_grad_kernel,
        grid=(count // block,),
        in_specs=[pl.BlockSpec((parts, block, width), lambda i: (0, i, 0)),
                  pl.BlockSpec((width, parts * width), lambda i: (0, 0), pipeline_mode=pl.Buffered(1)),
                  pl.BlockSpec((block, width), lambda i: (i, 0))],
        out_specs=pl.BlockSpec((block, width), lambda i: (i, 0)),
        out_shape=jax.ShapeDtypeStruct((count, width), F32),
        cost_estimate=pl.CostEstimate(flops=2 * count * width * parts * width, transcendentals=0,
                                      bytes_accessed=2 * (count + width) * parts * width + 8 * count * width),
        name="token_grad",
    )(grad, weight, rest)


def exchange(value, bit, devices):
    return lax.ppermute(value, AXES, [(i, i ^ bit) for i in range(devices)])


def tie(values, *after):
    return lax.optimization_barrier((values, after))[0]


def bits_of(devices):
    return [1 << k for k in range(devices.bit_length() - 1)][::-1]


def orders_of(devices):
    high = [b for b in bits_of(devices) if b >= 8]
    return ([1, 2, 4] + high[::-1], [1, 4, 2] + high[::-1])


def pick(value, index, axis):
    return lax.dynamic_index_in_dim(value, index, axis, keepdims=False)


class Summed:
    def __init__(self, grads, me, devices, colours):
        self.me, self.devices, self.colours = me, devices, colours
        self.bits = bits_of(devices)
        axis = len(self.bits) - 1
        mine = me & 1
        self.halves, self.got = [], []
        for grad in grads:
            whole = grad.reshape((2,) * len(self.bits) + (grad.shape[0] // devices, grad.shape[1]))
            self.halves.append(pick(whole, mine, axis))
            self.got.append(exchange(pick(whole, 1 - mine, axis), 1, devices))
        self.left = [[b for b in self.bits if b != 1] for _ in colours]
        self.orders = [list(o[1:]) for o in orders_of(devices)]
        self.states = None

    def step(self):
        if self.states is None:
            sums = [h.astype(F32) + g.astype(F32) for h, g in zip(self.halves, self.got)]
            self.states = [
                jnp.concatenate([sums[a][..., s:e] for a, s, e in colour], axis=-1)
                for colour in self.colours
            ]
        else:
            self.states = [k.astype(F32) + g.astype(F32) for k, g in zip(self.kept, self.got)]
        if not self.orders[0]:
            return False
        self.kept, self.got = [], []
        for i, state in enumerate(self.states):
            bit = self.orders[i].pop(0)
            axis = self.left[i].index(bit)
            self.left[i].remove(bit)
            mine = (self.me // bit) & 1
            low = state.astype(BF16)
            self.kept.append(pick(low, mine, axis))
            self.got.append(exchange(pick(low, 1 - mine, axis), bit, self.devices))
        return True

    def finish(self):
        while self.step():
            pass
        return self.states


def gather_rows(shard, me, devices, cuts):
    outs = []
    for order, (start, stop) in zip(orders_of(devices), cuts):
        state = shard[:, start:stop]
        done = []
        for bit in order[::-1]:
            got = exchange(state, bit, devices)
            axis = sum(1 for b in done if b > bit)
            done.append(bit)
            mine = ((me // bit) & 1) == 0
            state = jnp.stack(
                [jnp.where(mine, state, got), jnp.where(mine, got, state)], axis=axis
            )
        outs.append(state.reshape(devices * shard.shape[0], stop - start))
    return outs


def local(
    tokens, cotangent, segment_ids, valid_count, qkv_weight, qv_bias, out_weight, out_bias,
    norm_gain, norm_shift, in_weight, in_bias, back_weight, back_bias, final_gain, final_shift,
):
    head_index = lax.axis_index("heads")
    devices = lax.axis_size("rows") * lax.axis_size("heads")
    token_count, width = tokens.shape
    row_length = segment_ids.shape[1]
    rows = token_count // row_length
    shard = qkv_weight.shape[0]
    ff = in_weight.shape[1]
    small = [qv_bias[0], qv_bias[1], out_bias, norm_gain, norm_shift, in_bias, back_bias,
             final_gain, final_shift]
    sizes = [s.shape[0] for s in small]
    total = sum(sizes)
    lanes = -(-total // (shard * 128)) * 128
    packed = jnp.pad(jnp.concatenate(small), (0, shard * lanes - total)).reshape(shard, lanes)
    me = lax.axis_index("rows") * lax.axis_size("heads") + head_index
    joined = jnp.concatenate([qkv_weight, packed], axis=1)
    half = (joined.shape[1] // 256) * 128
    butterfly = shard % 8 == 0 and devices & (devices - 1) == 0 and devices >= 8
    if butterfly:
        first = jnp.concatenate(
            gather_rows(joined, me, devices, ((0, half), (half, joined.shape[1]))), axis=1
        )
    else:
        first = lax.all_gather(joined, AXES, axis=0, tiled=True)
    qkv_all = first[:, : 3 * width]
    vectors = first[:, 3 * width :].reshape(devices, shard * lanes)
    parts = []
    at = 0
    for n in sizes:
        parts.append(vectors[:, at : at + n].reshape(devices * n).astype(F32))
        at += n
    (q_bias, v_bias, out_bias_f, gain_f, shift_f, in_bias_f, back_bias_f, fgain_f, fshift_f) = parts
    table = jnp.stack([out_bias_f, gain_f, shift_f, back_bias_f, fgain_f, fshift_f,
                       fshift_f, fshift_f])
    group = ff // width
    turned = back_weight.reshape(group, shard, width).transpose(1, 0, 2).reshape(shard, ff)
    second = lax.all_gather(
        jnp.concatenate([in_weight, turned, out_weight], axis=1), AXES, axis=0, tiled=True
    )
    in_all = second[:, :ff]
    back_all = second[:, ff : 2 * ff].reshape(devices, shard, group, width)
    back_all = back_all.transpose(0, 2, 1, 3).reshape(ff, width)
    out_all = second[:, 2 * ff :]

    segments = lax.dynamic_slice(segment_ids, (head_index * rows, 0), (rows, row_length))
    counts = lax.dynamic_slice(valid_count, (head_index * rows,), (rows,))
    bias_full = jnp.concatenate([q_bias, jnp.zeros_like(q_bias), v_bias])
    proj = (jnp.dot(tokens, qkv_all, preferred_element_type=F32) + bias_full).astype(BF16)
    context, lse = attend_forward(proj, segments, counts)
    layer_out, low, n1, r1, act, g_pre, g_res2, g_ffn, sums2, g_in_bias = feed_call(
        context, tokens, cotangent, counts, table, in_bias_f[None], out_all, in_all, back_all, row_length
    )
    cast = lambda x: x.astype(BF16)
    tn = (((0,), (0,)), ((), ()))
    g_back = cast(dot(act, g_ffn, tn))
    if butterfly:
        ride_b = Summed([g_back], me, devices, [[(0, 0, width // 2)], [(0, width // 2, width)]])
        g_pre, g_res2 = tie((g_pre, g_res2), ride_b.got)
        ride_b.step()
    g_res1, g_attn, g_context, sums1 = back_call(g_pre, g_res2, n1, r1, table, in_all, out_all)
    if butterfly:
        low_t, g_pre_t, context_t, g_attn_t = tie((low, g_pre, context, g_attn), ride_b.got)
        ride_b.step()
    else:
        low_t, g_pre_t, context_t, g_attn_t = low, g_pre, context, g_attn
    g_in = cast(dot(low_t, g_pre_t, tn))
    g_out = cast(dot(context_t, g_attn_t, tn))
    if butterfly:
        cut = (ff + width) // 256 * 128
        ride_i = Summed([g_in, g_out], me, devices, [[(0, 0, cut)], [(0, cut, ff), (1, 0, width)]])
        g_context = tie(g_context, ride_i.got, ride_b.got)
        ride_i.step()
        ride_b.step()
    g_proj = attend_backward(proj, context, g_context, lse, segments, counts)
    if butterfly:
        g_proj = tie(g_proj, ride_i.got, ride_b.got)
        ride_i.step()
    g_qkv = weight_grad(tokens, g_proj)
    column = jnp.sum(g_proj.astype(F32), axis=1)
    g_small = [column[0], column[2], sums1[2], sums1[0], sums1[1], g_in_bias[0], sums2[2], sums2[0],
               sums2[1]]
    g_packed = jnp.concatenate([g.reshape(devices, -1) for g in g_small], axis=1)
    g_packed = jnp.pad(g_packed, ((0, 0), (0, shard * lanes - total))).astype(BF16)
    g_packed = g_packed.reshape(devices * shard, lanes)
    if butterfly:
        n = 3 * width + lanes
        ride_q = Summed([g_qkv, g_packed], me, devices,
                        [[(0, 0, half)], [(0, half, 3 * width), (1, 0, lanes)]])
        g_proj = tie(g_proj, ride_q.got, ride_i.got)
        ride_i.step()
        ride_q.step()
    grad_tokens = token_grad(g_proj, qkv_all, g_res1)
    if butterfly:
        g_back_own = jnp.concatenate(ride_b.finish(), axis=1)
        one, two = ride_i.finish()
        g_in_own = jnp.concatenate([one, two[:, : ff - cut]], axis=1)
        g_out_own = two[:, ff - cut :]
        one, two = ride_q.finish()
        g_qkv_own = jnp.concatenate([one, two[:, : 3 * width - half]], axis=1)
        mine = two[:, 3 * width - half :]
    else:
        give = lambda g: lax.psum_scatter(g, AXES, scatter_dimension=0, tiled=True).astype(F32)
        g_back_own, g_in_own, g_out_own = give(g_back), give(g_in), give(g_out)
        g_qkv_own, mine = give(g_qkv), give(g_packed)
    mine = mine.reshape(shard * lanes)
    own = []
    at = 0
    for n in sizes:
        own.append(mine[at : at + n])
        at += n
    return (
        layer_out, grad_tokens, g_qkv_own, jnp.stack([own[0], own[1]]), g_out_own, own[2], own[3],
        own[4], g_in_own, own[5], g_back_own, own[6], own[7], own[8],
    )


def solution(mesh):
    both = P(AXES, None)
    vec = P(AXES)
    in_specs = (both, both, P("rows", None), P("rows"), both, P(None, AXES), both, vec, vec, vec,
                both, vec, both, vec, vec, vec)
    out_specs = (both, both, both, P(None, AXES), both, vec, vec, vec, both, vec, both, vec, vec,
                 vec)
    return jax.shard_map(local, mesh=mesh, in_specs=in_specs, out_specs=out_specs, check_vma=False)
```

```python
import math
from functools import partial

import jax
import jax.numpy as jnp
from jax import lax
from jax.experimental import pallas as pl
from jax.experimental.pallas import tpu as pltpu
from jax.sharding import PartitionSpec as P

HEADS = 12
HEAD_DIM = 64
EPS = 1e-12
NEG = -1e30
AXES = ("rows", "heads")
F32 = jnp.float32
BF16 = jnp.bfloat16
NT = (((1,), (1,)), ((), ()))
NN = (((1,), (0,)), ((), ()))


def dot(a, b, dims=NN):
    return lax.dot_general(a, b, dims, preferred_element_type=F32)


def fill_mask(bias_ref, key_segment, query_segment, count):
    keys = lax.broadcasted_iota(jnp.int32, bias_ref.shape, 0)
    queries = lax.broadcasted_iota(jnp.int32, bias_ref.shape, 1)
    allowed = ((key_segment == query_segment) & (keys < count)) | (keys == queries)
    bias_ref[...] = jnp.where(allowed, 0.0, NEG)


def attend_forward_kernel(count_ref, kseg_ref, qseg_ref, q_ref, k_ref, v_ref, ctx_ref, lse_ref, bias_ref):
    row = pl.program_id(0)

    @pl.when(pl.program_id(1) == 0)
    def _():
        fill_mask(bias_ref, kseg_ref[0], qseg_ref[0], count_ref[row])

    for h in range(6):
        cols = slice(h * HEAD_DIM, (h + 1) * HEAD_DIM)
        query = q_ref[:, cols] * BF16(HEAD_DIM**-0.5)
        scores = dot(k_ref[:, cols], query, NT) + bias_ref[...]
        top = jnp.max(scores, axis=0, keepdims=True)
        exponent = jnp.exp(scores - top)
        total = jnp.sum(exponent, axis=0, keepdims=True)
        inverse = jnp.broadcast_to(1.0 / total, (HEAD_DIM, 512)).T
        context = dot(exponent.astype(BF16), v_ref[:, cols], (((0,), (0,)), ((), ())))
        ctx_ref[:, cols] = (context * inverse).astype(BF16)
        lse_ref[0, 0, h : h + 1, :] = top + jnp.log(total)


def attend_forward(proj, segments, counts):
    tokens, columns = proj.shape
    rows, length = segments.shape
    width = columns // 3
    pairs = width // 384
    block = lambda shift: pl.BlockSpec((length, 384), lambda r, p, c: (r, shift * pairs + p))
    return pl.pallas_call(
        attend_forward_kernel,
        grid_spec=pltpu.PrefetchScalarGridSpec(
            num_scalar_prefetch=1,
            grid=(rows, pairs),
            in_specs=[
                pl.BlockSpec((1, length, 1), lambda r, p, c: (r, 0, 0)),
                pl.BlockSpec((1, 1, length), lambda r, p, c: (r, 0, 0)),
                block(0), block(1), block(2),
            ],
            out_specs=[
                pl.BlockSpec((length, 384), lambda r, p, c: (r, p)),
                pl.BlockSpec((1, 1, 6, length), lambda r, p, c: (r, p, 0, 0)),
            ],
            scratch_shapes=[pltpu.VMEM((length, length), F32)],
        ),
        out_shape=[
            jax.ShapeDtypeStruct((tokens, width), BF16),
            jax.ShapeDtypeStruct((rows, pairs, 6, length), F32),
        ],
        cost_estimate=pl.CostEstimate(flops=8 * tokens * length * width, transcendentals=tokens * length * 12,
                                      bytes_accessed=8 * tokens * width),
        name="attend_forward",
    )(counts, segments[:, :, None], segments[:, None, :], proj, proj, proj)


def attend_backward_kernel(count_ref, kseg_ref, qseg_ref, q_ref, k_ref, v_ref, ctx_ref, gctx_ref, lse_ref,
                           g_ref, sums_ref, bias_ref):
    row = pl.program_id(0)
    fill_mask(bias_ref, kseg_ref[0], qseg_ref[0], count_ref[row])

    @pl.when(row == 0)
    def _():
        sums_ref[...] = jnp.zeros_like(sums_ref)

    key_t = k_ref[...].T
    product_t = (gctx_ref[...].astype(F32) * ctx_ref[...].astype(F32)).T
    scale = HEAD_DIM**-0.5
    for h in range(q_ref.shape[1] // HEAD_DIM):
        cols = slice(h * HEAD_DIM, (h + 1) * HEAD_DIM)
        query = q_ref[:, cols] * BF16(scale)
        scores = dot(k_ref[:, cols], query, NT) + bias_ref[...]
        probs = jnp.exp(scores - lse_ref[0, 0, h : h + 1, :])
        inner = jnp.sum(product_t[cols], axis=0, keepdims=True)
        g_probs = dot(v_ref[:, cols], gctx_ref[:, cols], NT)
        g_scores = (probs * (g_probs - inner)).astype(BF16)
        g_value = dot(probs.astype(BF16), gctx_ref[:, cols]).astype(BF16)
        g_query = (dot(key_t[cols], g_scores).T * scale).astype(BF16)
        g_ref[2, :, cols] = g_value
        g_ref[1, :, cols] = dot(g_scores, query).astype(BF16)
        g_ref[0, :, cols] = g_query
        sums_ref[0:1, cols] += jnp.sum(g_query.astype(F32), axis=0, keepdims=True)
        sums_ref[1:2, cols] += jnp.sum(g_value.astype(F32), axis=0, keepdims=True)


def attend_backward(proj, context, g_context, lse, segments, counts, part):
    tokens, columns = proj.shape
    rows, length = segments.shape
    width = columns // 3
    parts = lse.shape[1]
    size = width // parts
    block = lambda shift: pl.BlockSpec((length, size), lambda r, c: (r, shift * parts + part))
    return pl.pallas_call(
        attend_backward_kernel,
        grid_spec=pltpu.PrefetchScalarGridSpec(
            num_scalar_prefetch=1,
            grid=(rows,),
            in_specs=[
                pl.BlockSpec((1, length, 1), lambda r, c: (r, 0, 0)),
                pl.BlockSpec((1, 1, length), lambda r, c: (r, 0, 0)),
                block(0), block(1), block(2), block(0), block(0),
                pl.BlockSpec((1, 1, lse.shape[2], length), lambda r, c: (r, part, 0, 0)),
            ],
            out_specs=[pl.BlockSpec((3, length, size), lambda r, c: (0, r, 0)),
                       pl.BlockSpec((8, size), lambda r, c: (0, 0))],
            scratch_shapes=[pltpu.VMEM((length, length), F32)],
        ),
        out_shape=[jax.ShapeDtypeStruct((3, tokens, size), BF16), jax.ShapeDtypeStruct((8, size), F32)],
        cost_estimate=pl.CostEstimate(flops=20 * tokens * length * size, transcendentals=tokens * length * 6,
                                      bytes_accessed=16 * tokens * size),
        name="attend_backward",
    )(counts, segments[:, :, None], segments[:, None, :], proj, proj, proj, context, g_context, lse)


def project_kernel(tok_ref, wa_ref, wb_ref, proj_ref, table_ref, flip_ref):
    width, cut = wa_ref.shape

    @pl.when(pl.program_id(0) == 0)
    def _():
        flip_ref[...] = wb_ref[:, 3 * width - cut :].astype(F32).T
        table_ref[...] = flip_ref[0 : table_ref.shape[0]]

    first = dot(tok_ref[...], wa_ref[...])
    proj_ref[:, :width] = (first[:, :width] + flip_ref[0:1]).astype(BF16)
    proj_ref[:, width:cut] = first[:, width:].astype(BF16)
    second = dot(tok_ref[...], wb_ref[:, : 3 * width - cut])
    proj_ref[:, cut : 2 * width] = second[:, : 2 * width - cut].astype(BF16)
    proj_ref[:, 2 * width :] = (second[:, 2 * width - cut :] + flip_ref[1:2]).astype(BF16)


def project(tokens, wa, wb, block=256):
    count, width = tokens.shape
    return pl.pallas_call(
        project_kernel,
        grid=(count // block,),
        in_specs=[pl.BlockSpec((block, width), lambda i: (i, 0))]
        + [pl.BlockSpec(w.shape, lambda i: (0, 0), pipeline_mode=pl.Buffered(1)) for w in (wa, wb)],
        out_specs=[pl.BlockSpec((block, 3 * width), lambda i: (i, 0)), pl.BlockSpec((16, width), lambda i: (0, 0))],
        out_shape=[jax.ShapeDtypeStruct((count, 3 * width), BF16), jax.ShapeDtypeStruct((16, width), F32)],
        scratch_shapes=[pltpu.VMEM((128, width), F32)],
        cost_estimate=pl.CostEstimate(flops=6 * count * width * width, transcendentals=0,
                                      bytes_accessed=8 * count * width + 6 * width * width),
        name="project",
    )(tokens, wa, wb)


def mean(values):
    return jnp.mean(values, axis=-1, keepdims=True)


def add_rows(ref, rows):
    for i, value in enumerate(rows):
        ref[i : i + 1, :] += jnp.sum(value, axis=0, keepdims=True)


def feed_kernel(length, count_ref, ctx_ref, tok_ref, cot_ref, vec_ref, inw_ref, backw_ref, outw_ref,
                layer_ref, low_ref, n1_ref, r1_ref, act_ref, gpre_ref, gres_ref, gffn_ref, sums_ref, slope_ref):
    step = pl.program_id(0)
    block, width = tok_ref.shape
    groups = inw_ref.shape[1] // width

    @pl.when(step == 0)
    def _():
        sums_ref[...] = jnp.zeros_like(sums_ref)

    value = tok_ref[...].astype(F32) + (dot(ctx_ref[...], outw_ref[...]) + vec_ref[2:3])
    centered = value - mean(value)
    r1 = lax.rsqrt(mean(centered * centered) + EPS)
    n1 = centered * r1
    n1_ref[...] = n1.astype(BF16)
    r1_ref[...] = r1
    hidden = n1 * vec_ref[3:4] + vec_ref[4:5]
    low = hidden.astype(BF16)
    low_ref[...] = low
    feed = vec_ref[5:6] + hidden
    for m in range(groups):
        cols = slice(m * width, (m + 1) * width)
        pre = dot(low, inw_ref[:, cols]) + vec_ref[8 + m : 9 + m]
        cdf = 0.5 + 0.5 * lax.erf(pre * (0.5**0.5))
        act = (pre * cdf).astype(BF16)
        act_ref[:, cols] = act
        bell = jnp.exp(pre * pre * -0.5) * (1.0 / math.sqrt(2 * math.pi))
        slope_ref[:, cols] = (cdf + pre * bell).astype(BF16)
        feed = feed + dot(act, backw_ref[:, cols])
    centered = feed - mean(feed)
    r2 = lax.rsqrt(mean(centered * centered) + EPS)
    n2 = centered * r2
    start = (step * block) % length
    position = start + lax.broadcasted_iota(jnp.int32, (block, 1), 0)
    valid = (position < count_ref[(step * block) // length]).astype(F32)
    layer_ref[...] = ((n2 * vec_ref[6:7] + vec_ref[7:8]) * valid).astype(BF16)
    g_final = cot_ref[...].astype(F32) * valid
    g_n = g_final * vec_ref[6:7]
    g_res = r2 * (g_n - mean(g_n) - n2 * mean(g_n * n2))
    gres_ref[...] = g_res
    g_ffn = g_res.astype(BF16)
    gffn_ref[...] = g_ffn
    add_rows(sums_ref, [g_ffn.astype(F32), g_final * n2, g_final])
    for m in range(groups):
        cols = slice(m * width, (m + 1) * width)
        g_act = dot(g_ffn, backw_ref[:, cols], NT)
        g_pre = (g_act * slope_ref[:, cols].astype(F32)).astype(BF16)
        gpre_ref[:, cols] = g_pre
        sums_ref[3 + m : 4 + m, :] += jnp.sum(g_pre.astype(F32), axis=0, keepdims=True)


def feed_call(context, tokens, cotangent, counts, table, weights, ff, length, block=256):
    count, width = tokens.shape
    row = lambda n, dtype: (pl.BlockSpec((block, n), lambda i, c: (i, 0)), jax.ShapeDtypeStruct((count, n), dtype))
    once = dict(pipeline_mode=pl.Buffered(1))
    outs = [row(width, BF16), row(width, BF16), row(width, BF16), row(1, F32), row(ff, BF16), row(ff, BF16),
            row(width, F32), row(width, BF16),
            (pl.BlockSpec((8, width), lambda i, c: (0, 0)), jax.ShapeDtypeStruct((8, width), F32))]
    tok = row(width, BF16)[0]
    return pl.pallas_call(
        partial(feed_kernel, length),
        grid_spec=pltpu.PrefetchScalarGridSpec(
            num_scalar_prefetch=1,
            grid=(count // block,),
            in_specs=[tok, tok, tok, pl.BlockSpec(table.shape, lambda i, c: (0, 0), **once),
                      pl.BlockSpec((width, ff), lambda i, c: (0, 0), **once),
                      pl.BlockSpec((width, ff), lambda i, c: (0, 1), **once),
                      pl.BlockSpec((width, width), lambda i, c: (0, 2 * ff // width), **once)],
            out_specs=[o[0] for o in outs],
            scratch_shapes=[pltpu.VMEM((block, ff), BF16)],
        ),
        out_shape=[o[1] for o in outs],
        compiler_params=pltpu.CompilerParams(vmem_limit_bytes=56 << 20),
        cost_estimate=pl.CostEstimate(flops=2 * count * width * (width + 3 * ff), transcendentals=2 * count * ff,
                                      bytes_accessed=2 * count * (8 * width + 2 * ff) + 4 * width * ff),
        name="feed",
    )(counts, context, tokens, cotangent, table, weights, weights, weights)


def back_kernel(gpre_ref, gres_ref, n1_ref, r1_ref, vec_ref, inw_ref, outw_ref, gres1_ref, gattn_ref, gctx_ref, sums_ref):
    @pl.when(pl.program_id(0) == 0)
    def _():
        sums_ref[...] = jnp.zeros_like(sums_ref)

    g_hidden = gres_ref[...] + dot(gpre_ref[...], inw_ref[...], NT)
    n1 = n1_ref[...].astype(F32)
    g_m = g_hidden * vec_ref[3:4]
    g_res1 = r1_ref[...] * (g_m - mean(g_m) - n1 * mean(g_m * n1))
    gres1_ref[...] = g_res1
    g_attn = g_res1.astype(BF16)
    gattn_ref[...] = g_attn
    gctx_ref[...] = dot(g_attn, outw_ref[...], NT).astype(BF16)
    add_rows(sums_ref, [g_attn.astype(F32), g_hidden * n1, g_hidden])


def back_call(g_pre, g_res, n1, r1, table, weights, block=256):
    count, width = g_res.shape
    ff = g_pre.shape[1]
    row = lambda n, dtype: (pl.BlockSpec((block, n), lambda i: (i, 0)), jax.ShapeDtypeStruct((count, n), dtype))
    once = dict(pipeline_mode=pl.Buffered(1))
    outs = [row(width, F32), row(width, BF16), row(width, BF16),
            (pl.BlockSpec((8, width), lambda i: (0, 0)), jax.ShapeDtypeStruct((8, width), F32))]
    return pl.pallas_call(
        back_kernel,
        grid=(count // block,),
        in_specs=[row(ff, BF16)[0], row(width, F32)[0], row(width, BF16)[0], row(1, F32)[0],
                  pl.BlockSpec(table.shape, lambda i: (0, 0), **once),
                  pl.BlockSpec((width, ff), lambda i: (0, 0), **once),
                  pl.BlockSpec((width, width), lambda i: (0, 2 * ff // width), **once)],
        out_specs=[o[0] for o in outs],
        out_shape=[o[1] for o in outs],
        compiler_params=pltpu.CompilerParams(vmem_limit_bytes=48 << 20),
        cost_estimate=pl.CostEstimate(flops=2 * count * width * (width + ff), transcendentals=0,
                                      bytes_accessed=2 * count * (8 * width + ff) + 2 * width * ff),
        name="back",
    )(g_pre, g_res, n1, r1, table, weights, weights)


def weight_grad_kernel(left_ref, right_ref, out_ref):
    out_ref[...] = dot(left_ref[...], right_ref[0]).astype(BF16)


def weight_grad(left, right):
    rows, count = left.shape
    parts, _, columns = right.shape
    return pl.pallas_call(
        weight_grad_kernel,
        grid=(parts,),
        in_specs=[pl.BlockSpec((rows, count), lambda k: (0, 0), pipeline_mode=pl.Buffered(1)),
                  pl.BlockSpec((1, count, columns), lambda k: (k, 0, 0))],
        out_specs=pl.BlockSpec((rows, columns), lambda k: (0, k)),
        out_shape=jax.ShapeDtypeStruct((rows, parts * columns), BF16),
        cost_estimate=pl.CostEstimate(flops=2 * count * rows * parts * columns, transcendentals=0,
                                      bytes_accessed=2 * (count * rows + (count + rows) * parts * columns)),
        name="weight_grad",
    )(left, right)


def token_grad_kernel(ga_ref, gb_ref, wa_ref, wb_ref, rest_ref, out_ref):
    total = rest_ref[...]
    size = ga_ref.shape[2]
    for k in range(6):
        grad = (ga_ref, gb_ref)[k % 2][k // 2]
        weight = (wa_ref, wb_ref)[k // 3][:, (k % 3) * size : (k % 3 + 1) * size]
        total = total + dot(grad, weight, NT)
    out_ref[...] = total


def token_grad(ga, gb, wa, wb, rest, block=256):
    parts, count, size = ga.shape
    width = rest.shape[1]
    return pl.pallas_call(
        token_grad_kernel,
        grid=(count // block,),
        in_specs=[pl.BlockSpec((parts, block, size), lambda i: (0, i, 0))] * 2
        + [pl.BlockSpec(w.shape, lambda i: (0, 0), pipeline_mode=pl.Buffered(1)) for w in (wa, wb)]
        + [pl.BlockSpec((block, width), lambda i: (i, 0))],
        out_specs=pl.BlockSpec((block, width), lambda i: (i, 0)),
        out_shape=jax.ShapeDtypeStruct((count, width), F32),
        cost_estimate=pl.CostEstimate(flops=6 * count * width * width, transcendentals=0,
                                      bytes_accessed=6 * (count + width) * width + 8 * count * width),
        name="token_grad",
    )(ga, gb, wa, wb, rest)


def exchange(value, bit, devices):
    return lax.ppermute(value, AXES, [(i, i ^ bit) for i in range(devices)])


def tie(values, *after):
    return lax.optimization_barrier((values, after))[0]


def bits_of(devices):
    return [1 << k for k in range(devices.bit_length() - 1)][::-1]


def order_of(devices, flip):
    high = [b for b in bits_of(devices) if b >= 8]
    return ([1, 4, 2] if flip else [1, 2, 4]) + high[::-1]


def pick(value, index, axis):
    return lax.dynamic_index_in_dim(value, index, axis, keepdims=False)


class Summed:
    def __init__(self, grads, me, devices, flip):
        self.me, self.devices = me, devices
        self.left = bits_of(devices)
        self.order = order_of(devices, flip)
        self.shapes = [(g.shape[0], g.shape[2]) for g in grads]
        self.states = [
            g.reshape((g.shape[0],) + (2,) * len(self.left) + (g.shape[1] // devices, g.shape[2]))
            for g in grads
        ]
        self.send()

    def send(self):
        bit = self.order.pop(0)
        axis = 1 + self.left.index(bit)
        self.left.remove(bit)
        mine = (self.me // bit) & 1
        self.kept = [pick(s, mine, axis) for s in self.states]
        self.sent = [pick(s, 1 - mine, axis) for s in self.states]
        self.got = [exchange(s, bit, self.devices) for s in self.sent]

    def wait_for(self, *after):
        self.got = tie(self.got, *after)

    def step(self):
        sums = [k.astype(F32) + g.astype(F32) for k, g in zip(self.kept, self.got)]
        if not self.order:
            self.states = sums
            return False
        if len(sums) > 1:
            sums = [jnp.concatenate(
                [jnp.moveaxis(s, 0, -2).reshape(s.shape[1:-1] + (s.shape[0] * s.shape[-1],)) for s in sums],
                axis=-1)[None]]
        self.states = [s.astype(BF16) for s in sums]
        self.send()
        return True

    def finish(self):
        while self.step():
            pass
        return self.states[0]


def gather_rows(shard, me, devices, flip):
    state = shard
    done = []
    for bit in order_of(devices, flip)[::-1]:
        got = exchange(state, bit, devices)
        axis = sum(1 for b in done if b > bit)
        done.append(bit)
        mine = ((me // bit) & 1) == 0
        state = jnp.stack([jnp.where(mine, state, got), jnp.where(mine, got, state)], axis=axis)
    return state.reshape(devices * shard.shape[0], shard.shape[1])


def local(
    tokens, cotangent, segment_ids, valid_count, qkv_weight, qv_bias, out_weight, out_bias,
    norm_gain, norm_shift, in_weight, in_bias, back_weight, back_bias, final_gain, final_shift,
):
    head_index = lax.axis_index("heads")
    devices = lax.axis_size("rows") * lax.axis_size("heads")
    me = lax.axis_index("rows") * lax.axis_size("heads") + head_index
    token_count, width = tokens.shape
    row_length = segment_ids.shape[1]
    rows = token_count // row_length
    shard = qkv_weight.shape[0]
    ff = in_weight.shape[1]
    group = ff // width
    cut = 3 * width // 2
    butterfly = shard % 8 == 0 and devices & (devices - 1) == 0 and devices >= 8

    small = jnp.concatenate([v.reshape(-1, shard) for v in (
        qv_bias, out_bias, norm_gain, norm_shift, back_bias, final_gain, final_shift, in_bias)], axis=0)
    small = jnp.pad(small.T, ((0, 0), (0, 128 - small.shape[0])))
    shard_a, shard_b = qkv_weight[:, :cut], jnp.concatenate([qkv_weight[:, cut:], small], axis=1)
    inner = in_weight.reshape(shard, devices, group, shard).transpose(0, 2, 1, 3).reshape(shard, ff)
    turned = back_weight.reshape(group, shard, width).transpose(1, 0, 2).reshape(shard, ff)
    weights = lax.all_gather(
        jnp.concatenate([inner, turned, out_weight], axis=1), AXES, axis=0, tiled=True
    )
    if butterfly:
        wa = gather_rows(shard_a, me, devices, False)
        wb = gather_rows(shard_b, me, devices, True)
    else:
        first = lax.all_gather(jnp.concatenate([shard_a, shard_b], axis=1), AXES, axis=0, tiled=True)
        wa, wb = first[:, :cut], first[:, cut:]

    segments = lax.dynamic_slice(segment_ids, (head_index * rows, 0), (rows, row_length))
    counts = lax.dynamic_slice(valid_count, (head_index * rows,), (rows,))
    tokens_t = tokens.T
    proj, table = project(tokens, wa, wb)
    context, lse = attend_forward(proj, segments, counts)
    layer_out, low, n1, r1, act, g_pre, g_res2, g_ffn, sums2 = feed_call(
        context, tokens, cotangent, counts, table, weights, ff, row_length
    )
    tn = (((0,), (0,)), ((), ()))
    g_in = dot(low, g_pre, tn).astype(BF16)[None]
    if butterfly:
        ride_i = Summed([g_in], me, devices, True)
        act, g_ffn = tie((act, g_ffn), ride_i.sent)
    g_back = dot(act, g_ffn, tn).astype(BF16).reshape(group, width, width)
    if butterfly:
        ride_b = Summed([g_back], me, devices, False)
        ride_i.wait_for(ride_b.sent)
        ride_i.step()
        ride_b.step()
        g_pre, g_res2 = tie((g_pre, g_res2), ride_i.sent, ride_b.sent)
    g_res1, g_attn, g_context, sums1 = back_call(g_pre, g_res2, n1, r1, table, weights)
    g_out = dot(context, g_attn, tn).astype(BF16)[None]
    ga, suma = attend_backward(proj, context, g_context, lse, segments, counts, 0)
    g_one = weight_grad(tokens_t, ga)[None]
    if butterfly:
        ride_i.wait_for(ga)
        ride_b.wait_for(ga)
        ride_i.step()
        ride_b.step()
        ride_1 = Summed([g_one, g_out], me, devices, False)
        g_context = tie(g_context, ride_i.sent, ride_b.sent, ride_1.sent)
    gb, sumb = attend_backward(proj, context, g_context, lse, segments, counts, 1)
    g_two = weight_grad(tokens_t, gb)[None]
    heads = jnp.concatenate([suma, sumb], axis=1)
    g_small = jnp.concatenate([heads[:2], sums1[:3], sums2[: 3 + group]], axis=0)
    g_small = jnp.pad(g_small, ((0, 128 - g_small.shape[0]), (0, 0))).T.astype(BF16)[None]
    g_res1_t = g_res1
    if butterfly:
        ride_i.wait_for(gb)
        ride_b.wait_for(gb)
        ride_1.wait_for(gb)
        ride_i.step()
        ride_b.step()
        ride_1.step()
        ride_2 = Summed([g_two, g_small], me, devices, True)
        g_res1_t = tie(g_res1, ride_i.sent, ride_b.sent, ride_1.sent, ride_2.sent)
    grad_tokens = token_grad(ga, gb, wa, wb, g_res1_t)
    size = width // 2
    if butterfly:
        for ride in (ride_i, ride_b, ride_1, ride_2):
            ride.wait_for(grad_tokens)
        two = ride_2.step()
        own_in = ride_i.finish()[0]
        own_back = ride_b.finish()
        own_1 = ride_1.finish()[0]
        own_2 = ride_2.finish()[0]
        own_out, mine = own_1[:, 3 * size :], own_2[:, 3 * size :]
    else:
        give = lambda g: lax.psum_scatter(g, AXES, scatter_dimension=1, tiled=True).astype(F32)
        own_in, own_back, own_out = give(g_in)[0], give(g_back), give(g_out)[0]
        own_1, own_2, mine = give(g_one)[0], give(g_two)[0], give(g_small)[0]
    own_in = own_in.reshape(shard, group, devices, shard).transpose(0, 2, 1, 3).reshape(shard, ff)
    own_qkv = jnp.concatenate(
        [(own_1, own_2)[k % 2][:, (k // 2) * size : (k // 2 + 1) * size] for k in range(6)], axis=1)
    vec = mine.T
    return (
        layer_out, grad_tokens, own_qkv, vec[:2], own_out, vec[2], vec[3], vec[4], own_in,
        vec[8 : 8 + group].reshape(group * shard), own_back.reshape(group * shard, width), vec[5], vec[6], vec[7],
    )


def solution(mesh):
    both = P(AXES, None)
    vec = P(AXES)
    in_specs = (both, both, P("rows", None), P("rows"), both, P(None, AXES), both, vec, vec, vec,
                both, vec, both, vec, vec, vec)
    out_specs = (both, both, both, P(None, AXES), both, vec, vec, vec, both, vec, both, vec, vec,
                 vec)
    return jax.shard_map(local, mesh=mesh, in_specs=in_specs, out_specs=out_specs, check_vma=False)
```
